32 devices in a mesh: gx: 4 (over y, x), gy: 4 (over z), gz: 2 (over core).
Axes of the slice: x: 2, y: 2, z: 4, core: 2. Of those that a mesh axis runs over, the one named last changes fastest.
Arguments:
- rhs: float32 [7, 7, 7, 4, 16, 256], P(None, None, None, 'gx', 'gy', 'gz'), may hold values from -6 to 6
- orders: int32 [4, 16, 256], P('gx', 'gy', 'gz'), may hold values from 3 to 6
Outputs:
- smoothed: float32 [7, 7, 7, 4, 16, 256], P(None, None, None, 'gx', 'gy', 'gz')
- coarse_residual: float32 [4, 16, 256], P('gx', 'gy')
The draws below stay inside these ranges and needn't reach their ends.
All inputs are finite; a program needn't handle non-finite values.
Results may differ from the reference program's by a relative error of at most 0.00016.
Values sent between devices are 32-bit elements; how exact they have to be, the bound alone decides.
A program may use at most 64 MiB of HBM per device.

```python
import jax
import jax.numpy as jnp
import numpy as np
from jax import lax

MODES = 7
NX = 4
NY = 16
NZ = 256


def set_ends(drawn, own_key, smallest, largest):
    dims = drawn.shape
    spot = [jax.random.randint(jax.random.fold_in(own_key, axis), (), 0, dims[axis]) for axis in range(len(dims))]
    drawn = drawn.at[tuple(spot)].set(smallest)
    longest = dims.index(max(dims))
    spot[longest] = (spot[longest] + 1) % dims[longest]
    return drawn.at[tuple(spot)].set(largest)


def block_levels(key, dims, pieces, smallest, largest):
    factor_of, own = 1.0, jax.random.fold_in(key, 6)
    for dim, blocks in pieces:
        draws = jnp.exp(jax.random.uniform(jax.random.fold_in(own, dim), (blocks,), jnp.float32, smallest / len(pieces), largest / len(pieces)))
        factor_of = factor_of * jnp.repeat(draws, dims[dim] // blocks).reshape([-1 if axis == dim else 1 for axis in range(len(dims))])
    return factor_of


def scatter_about(stream_key, shape, width, most, shards=(), dtype=jnp.bfloat16):
    values = jax.random.normal(stream_key, shape, jnp.float32) * width
    if len(shards) > 0:
        values = block_levels(stream_key, shape, shards, -0.22, 0.18) * values
    return jnp.clip(values, min=-most, max=most).astype(dtype)


def setup_inputs(seed: int = 0) -> dict:
    key_list = jax.random.split(jax.random.key(seed), 3)
    return {
        "rhs": scatter_about(key_list[0], (MODES, MODES, MODES, NX, NY, NZ), 1.0, 6.0, ((3, 4), (4, 4), (5, 2)), jnp.float32),
        "orders": set_ends(jax.random.randint(key_list[1], (NX, NY, NZ), 3, 7), jax.random.fold_in(key_list[1], 1), 3, 6).astype(jnp.int32),
    }


PENALTY = 49.0
EIGEN_HIGH = 2.4
EIGEN_LOW = 0.24
PRECISE = lax.Precision.HIGHEST

def basis_tables():
    degree = np.arange(7)
    normed = np.sqrt((2.0 * degree + 1.0) / 2.0)
    smaller = np.minimum(degree[:, None], degree[None, :])
    parity = (degree[:, None] + degree[None, :]) % 2 == 0
    stiffness = np.where(parity, normed[:, None] * normed[None, :] * smaller * (smaller + 1), 0.0)
    signs = (-1.0) ** degree
    slope = normed * degree * (degree + 1) / 2.0
    traces = np.stack([normed * signs, -slope * signs, normed, slope])
    stiff_diag = normed * normed * degree * (degree + 1)
    one_axis = stiff_diag + 2.0 * (PENALTY * normed * normed - normed * slope)
    diagonal = (one_axis[:, None, None] + one_axis[None, :, None] + one_axis[None, None, :]) / PENALTY
    highest = np.maximum(np.maximum(degree[:, None, None], degree[None, :, None]), degree[None, None, :])
    third = np.sqrt(1.5) / 3.0
    vertex = np.array([[np.sqrt(0.5), np.sqrt(0.5)], [-third, third]])
    return (stiffness, traces, diagonal, highest, vertex)

def face_stack(field, direction, traces):
    return jnp.stack([jnp.tensordot(traces[row], field, axes=(0, direction), precision=PRECISE) for row in range(4)])

def place(vector, plane, direction):
    return jnp.moveaxis(vector.reshape((7,) + (1,) * plane.ndim) * plane[None], 0, direction)

def middle(array, axis_cells, start):
    return lax.slice_in_dim(array, start, start + array.shape[axis_cells] - 2, axis=axis_cells)

def flux(extended, direction, traces):
    axis_cells = 3 + direction
    own = middle(extended, axis_cells, 1)
    lower = middle(extended, axis_cells, 0)
    upper = middle(extended, axis_cells, 2)
    jump_up = own[2] - upper[0]
    mean_up = 0.5 * (own[3] + upper[1])
    jump_low = lower[2] - own[0]
    mean_low = 0.5 * (lower[3] + own[1])
    result = place(traces[2], PENALTY * jump_up - mean_up, direction) - 0.5 * place(traces[3], jump_up, direction)
    return result + place(traces[0], mean_low - PENALTY * jump_low, direction) - 0.5 * place(traces[1], jump_low, direction)

def rim_stacks(padded, traces):
    stacks = []
    for direction in range(3):
        index = [slice(None)] * 6
        for other in range(3):
            if other != direction:
                index[3 + other] = slice(1, -1)
        stacks.append(face_stack(padded[tuple(index)], direction, traces))
    return stacks

def operate(field, mask, stacks, stiffness, traces):
    total = jnp.zeros_like(field)
    for direction in range(3):
        total = total + jnp.moveaxis(jnp.tensordot(stiffness, field, axes=(1, direction), precision=PRECISE), 0, direction)
        total = total + flux(stacks[direction], direction, traces)
    return mask * total / PENALTY

def carry_global(pair, axis_cells):
    leading = pair[1]
    count = leading.shape[axis_cells]
    moved = jnp.concatenate([jnp.zeros_like(lax.slice_in_dim(leading, 0, 1, axis=axis_cells)), lax.slice_in_dim(leading, 0, count - 1, axis=axis_cells)], axis=axis_cells)
    return pair[0] + moved

def reference(rhs, orders):
    tables = basis_tables()
    stiffness = jnp.asarray(tables[0], jnp.float32)
    traces = jnp.asarray(tables[1], jnp.float32)
    diagonal = jnp.asarray(tables[2], jnp.float32)
    highest = jnp.asarray(tables[3], jnp.int32)
    vertex = jnp.asarray(tables[4], jnp.float32)
    mask = (highest[:, :, :, None, None, None] <= orders[None, None, None]).astype(jnp.float32)
    inv_diag = mask / diagonal[:, :, :, None, None, None]

    def apply(field):
        padded = jnp.pad(field, ((0, 0),) * 3 + ((1, 1),) * 3)
        return operate(field, mask, rim_stacks(padded, traces), stiffness, traces)
    theta = 0.5 * (EIGEN_HIGH + EIGEN_LOW)
    delta = 0.5 * (EIGEN_HIGH - EIGEN_LOW)
    rho_first = delta / theta
    rho_second = 1.0 / (2.0 * theta / delta - rho_first)
    forcing = mask * rhs
    first = inv_diag * forcing / theta
    resid_one = forcing - apply(first)
    smoothed = first + (rho_second * rho_first * first + 2.0 * rho_second / delta * (inv_diag * resid_one))
    resid_two = forcing - apply(smoothed)
    corner = jnp.einsum('ai,bj,ck,abcxyz->ijkxyz', vertex, vertex, vertex, resid_two[:2, :2, :2], precision=PRECISE)
    along_x = carry_global(corner, 2)
    along_y = carry_global(along_x, 2)
    along_z = carry_global(along_y, 2)
    inside_x = (jnp.arange(NX) > 0).astype(jnp.float32)
    inside_y = (jnp.arange(NY) > 0).astype(jnp.float32)
    inside_z = (jnp.arange(NZ) > 0).astype(jnp.float32)
    interior = inside_x[:, None, None] * inside_y[None, :, None] * inside_z[None, None, :]
    return (smoothed, along_z * interior)
```

```python
import functools

import jax
import jax.numpy as jnp
import numpy as np
from jax import lax
from jax.experimental import pallas as pl
from jax.experimental.pallas import tpu as pltpu
from jax.sharding import PartitionSpec as P

PENALTY = 49.0
EIGEN_HIGH = 2.4
EIGEN_LOW = 0.24
MODES = 7
MESH = pl.DeviceIdType.MESH


def tables():
    degree = np.arange(MODES)
    normed = np.sqrt((2.0 * degree + 1.0) / 2.0)
    smaller = np.minimum(degree[:, None], degree[None, :])
    parity = (degree[:, None] + degree[None, :]) % 2 == 0
    stiffness = np.where(parity, normed[:, None] * normed[None, :] * smaller * (smaller + 1), 0.0)
    signs = (-1.0) ** degree
    slope = normed * degree * (degree + 1) / 2.0
    low, low_slope = normed * signs, -slope * signs
    own = stiffness + np.outer(normed, PENALTY * normed - 0.5 * slope) - 0.5 * np.outer(slope, normed)
    own = own + np.outer(low, PENALTY * low + 0.5 * low_slope) + 0.5 * np.outer(low_slope, low)
    one_axis = normed * normed * degree * (degree + 1) + 2.0 * (
        PENALTY * normed * normed - normed * slope
    )
    diagonal = (
        one_axis[:, None, None] + one_axis[None, :, None] + one_axis[None, None, :]
    ) / PENALTY
    return (
        own / PENALTY,
        0.5 * slope - PENALTY * normed,
        0.5 * normed,
        normed / PENALTY,
        slope / PENALTY,
        diagonal,
    )


OWN, JUMP, HALF, VALUE, SLOPE, DIAGONAL = tables()
THETA = 0.5 * (EIGEN_HIGH + EIGEN_LOW)
DELTA = 0.5 * (EIGEN_HIGH - EIGEN_LOW)
RHO_FIRST = DELTA / THETA
RHO_SECOND = 1.0 / (2.0 * THETA / DELTA - RHO_FIRST)
KEEP = 1.0 + RHO_SECOND * RHO_FIRST
STEP = 2.0 * RHO_SECOND / DELTA * THETA


def combine(weights, values):
    total = None
    for weight, value in zip(weights, values):
        term = value * float(weight)
        total = term if total is None else total + term
    return total


def traces(values):
    even, odd = values[0::2], values[1::2]
    jump_even, jump_odd = combine(JUMP[0::2], even), combine(JUMP[1::2], odd)
    half_even, half_odd = combine(HALF[0::2], even), combine(HALF[1::2], odd)
    down = (jump_even - jump_odd, half_even - half_odd)
    up = (jump_even + jump_odd, half_even + half_odd)
    return down, up


def own_row(row, values):
    start = row % 2
    return combine(OWN[row, start::2], values[start::2])


def face_terms(from_up, from_down):
    both = (from_up[0] + from_down[0], from_up[1] + from_down[1])
    apart = (from_up[0] - from_down[0], from_up[1] - from_down[1])

    def term(mode):
        pair = both if mode % 2 == 0 else apart
        if mode == 0:
            return pair[0] * float(VALUE[0])
        return pair[0] * float(VALUE[mode]) + pair[1] * float(SLOPE[mode])

    return term


def vertex_pair(zero, one):
    flat, tilt = np.sqrt(0.5) * zero, (np.sqrt(1.5) / 3.0) * one
    return flat - tilt, flat + tilt


def kernel(
    sizes, cells_y, cells_z, rhs_hbm, orders_ref, table_ref, out_hbm, coarse_ref,
    rhs, first, acc, smooth,
    xs, xr, ys, yr, zs, zr, y_up, y_down,
    xs2, xr2, ys2, yr2, zs2, zr2, y_up2, y_down2, acc2, shift_buf,
    main, top, main_in, top_in,
    local_sem, send_sem, recv_sem,
):
    nx, ny, nz = sizes
    x, y, z = lax.axis_index("gx"), lax.axis_index("gy"), lax.axis_index("gz")
    barrier = pltpu.get_barrier_semaphore()

    def neighbour(axis, sign):
        here = (x, y, z)[axis]
        to = [x, y, z]
        to[axis] = here + sign
        back = [x, y, z]
        back[axis] = here - sign
        below, above = here > 0, here < sizes[axis] - 1
        return (tuple(to), below if sign < 0 else above, tuple(back), above if sign < 0 else below)

    halos = [neighbour(axis, sign) for axis in range(3) for sign in (-1, 1)]
    always = x >= 0
    carries = []
    for i in range(2):
        for j in range(2):
            for r in range(nz):
                if i == 0 and j == 0 and r == 0:
                    continue
                to = (x + i, y + j, lax.rem(z + r, nz))
                source = lax.rem(z - r + nz, nz)
                back = (x - i, y - j, source)
                ok_to, ok_from = always, always
                if i:
                    ok_to, ok_from = ok_to & (x < nx - 1), ok_from & (x > 0)
                if j:
                    ok_to, ok_from = ok_to & (y < ny - 1), ok_from & (y > 0)
                carries.append((to, ok_to, back, ok_from, i, j, source))

    expected = jnp.int32(0)
    for entry in halos + carries:
        to, ok_to, back, ok_from = entry[:4]

        @pl.when(ok_from)
        def _(back=back):
            pl.semaphore_signal(barrier, inc=1, device_id=back, device_id_type=MESH)

        expected = expected + jnp.where(ok_to, 1, 0).astype(jnp.int32)

    load = pltpu.make_async_copy(rhs_hbm, rhs, local_sem.at[0])
    load.start()

    def remote(src, dst, slot, to):
        return pltpu.make_async_remote_copy(
            src_ref=src, dst_ref=dst, send_sem=send_sem.at[slot], recv_sem=recv_sem.at[slot],
            device_id=to, device_id_type=MESH,
        )

    def start(index, slot, src, dst):
        to, ok_to = halos[index][:2]

        @pl.when(ok_to)
        def _():
            remote(src, dst, slot, to).start()

    def receive(index, slot, src, dst):
        to, _, _, ok_from = halos[index]

        @pl.when(ok_from)
        def _():
            remote(src, dst, slot, to).wait_recv()

    def finish(index, slot, src, dst):
        to, ok_to = halos[index][:2]

        @pl.when(ok_to)
        def _():
            remote(src, dst, slot, to).wait_send()

    stages = (((xs, xr), (ys, yr), (zs, zr)), ((xs2, xr2), (ys2, yr2), (zs2, zr2)))

    def over(action, stage, axis):
        src, dst = stages[stage][axis]
        for side in range(2):
            index = 2 * axis + side
            action(index, 6 * stage + index, src.at[side], dst.at[side])

    for stage in range(2):
        for axis in range(3):
            for side in range(2):
                dst = stages[stage][axis][1]

                @pl.when(jnp.logical_not(halos[2 * axis + side][3]))
                def _(dst=dst, side=side):
                    dst[side] = jnp.zeros(dst.shape[1:], jnp.float32)

    orders = orders_ref[0]
    tile = (MODES, cells_y, cells_z)
    last_mode = lax.broadcasted_iota(jnp.int32, tile, 0)
    lane = lax.broadcasted_iota(jnp.int32, (1, 1, cells_z), 2)
    load.wait()

    def active(a, b):
        return jnp.maximum(jnp.maximum(a, b), last_mode) <= orders[None]

    def loop(body):
        def step(index, carry):
            body(index)
            return carry

        lax.fori_loop(0, MODES, step, 0)

    def x_traces(b):
        values = []
        for a in range(MODES):
            value = jnp.where(active(a, b), table_ref[a, b] * rhs[a, b], 0.0)
            first[a, b] = value
            values.append(value)
        sides = traces(values)
        for side in range(2):
            for kind in range(2):
                xs[side, kind, b] = sides[side][kind]

    loop(x_traces)
    pl.semaphore_wait(barrier, expected)
    over(start, 0, 0)

    def y_faces(a, values, send, up_buf, down_buf):
        down, up = traces(values)
        for kind in range(2):
            up_buf[kind, a, :, 0:cells_y, :] = down[kind]
            down_buf[kind, a, :, 1 : cells_y + 1, :] = up[kind]
            send[0, kind, a] = down[kind][:, 0:1, :]
            send[1, kind, a] = up[kind][:, cells_y - 1 : cells_y, :]

    def y_neighbours(a, received, up_buf, down_buf):
        for kind in range(2):
            up_buf[kind, a, :, cells_y : cells_y + 1, :] = received[0, kind, a]
            down_buf[kind, a, :, 0:1, :] = received[1, kind, a]
        return face_terms(
            [up_buf[kind, a, :, 1 : cells_y + 1, :] for kind in range(2)],
            [down_buf[kind, a, :, 0:cells_y, :] for kind in range(2)],
        )

    def z_faces(a, values, send):
        sides = traces(values)
        for side in range(2):
            for kind in range(2):
                send[side, kind, a] = sides[side][kind]

    def z_neighbours(a, send, received):
        def moved(side, kind, edge, amount):
            picked = jnp.where(lane == edge, received[side, kind, a], send[side, kind, a])
            return pltpu.roll(picked, amount, 2)

        return face_terms(
            [moved(0, kind, 0, cells_z - 1) for kind in range(2)],
            [moved(1, kind, cells_z - 1, 1) for kind in range(2)],
        )

    loop(lambda a: z_faces(a, [first[a, :, e] for e in range(MODES)], zs))
    over(start, 0, 2)
    loop(lambda a: y_faces(a, [first[a, b] for b in range(MODES)], ys, y_up, y_down))
    over(start, 0, 1)

    def x_own(b):
        values = [first[a, b] for a in range(MODES)]
        for a in range(MODES):
            acc[a, b] = own_row(a, values)

    def y_own(a):
        values = [first[a, b] for b in range(MODES)]
        for b in range(MODES):
            acc[a, b] += own_row(b, values)

    def z_own(a):
        values = [first[a, :, e] for e in range(MODES)]
        for e in range(MODES):
            acc[a, :, e] += own_row(e, values)

    loop(x_own)
    loop(y_own)
    loop(z_own)

    over(receive, 0, 2)

    def z_flux(a):
        term = z_neighbours(a, zs, zr)
        for e in range(MODES):
            acc[a, :, e] += term(e)

    loop(z_flux)
    over(receive, 0, 1)

    def y_flux(a):
        term = y_neighbours(a, yr, y_up, y_down)
        for b in range(MODES):
            acc[a, b] += term(b)

    loop(y_flux)
    over(receive, 0, 0)

    def x_flux(b):
        term = face_terms(
            [xr[0, kind, b] for kind in range(2)], [xr[1, kind, b] for kind in range(2)]
        )
        for a in range(MODES):
            right = rhs[a, b]
            total = acc[a, b] + term(a)
            value = table_ref[a, b] * (KEEP * right + STEP * (right - total))
            smooth[a, b] = jnp.where(active(a, b), value, 0.0)

    loop(x_flux)
    store = pltpu.make_async_copy(smooth, out_hbm, local_sem.at[1])
    store.start()

    for b in range(2):
        values = [smooth[a, b, 0:2] for a in range(MODES)]
        sides = traces(values)
        for side in range(2):
            for kind in range(2):
                xs2[side, kind, b] = sides[side][kind]
    over(start, 1, 0)
    for a in range(2):
        y_faces(a, [smooth[a, b, 0:2] for b in range(MODES)], ys2, y_up2, y_down2)
    over(start, 1, 1)
    for a in range(2):
        z_faces(a, [smooth[a, 0:2, e] for e in range(MODES)], zs2)
    over(start, 1, 2)
    for b in range(2):
        values = [smooth[a, b, 0:2] for a in range(MODES)]
        for a in range(2):
            acc2[a, b] = own_row(a, values)
    for a in range(2):
        values = [smooth[a, b, 0:2] for b in range(MODES)]
        for b in range(2):
            acc2[a, b] += own_row(b, values)
        values = [smooth[a, 0:2, e] for e in range(MODES)]
        for e in range(2):
            acc2[a, :, e] += own_row(e, values)
    over(receive, 1, 2)
    for a in range(2):
        term = z_neighbours(a, zs2, zr2)
        for e in range(2):
            acc2[a, :, e] += term(e)
    over(receive, 1, 1)
    for a in range(2):
        term = y_neighbours(a, yr2, y_up2, y_down2)
        for b in range(2):
            acc2[a, b] += term(b)
    over(receive, 1, 0)
    for b in range(2):
        term = face_terms(
            [xr2[0, kind, b] for kind in range(2)], [xr2[1, kind, b] for kind in range(2)]
        )
        for a in range(2):
            acc2[a, b] += term(a)

    resid = {}
    for a in range(2):
        for b in range(2):
            for e in range(2):
                left = rhs[a, b, e] - acc2[a, b, e]
                resid[a, b, e] = jnp.where(orders >= max(a, b, e), left, 0.0)
    for axis in range(3):
        done = {}
        for key in resid:
            if key[axis] == 0:
                other = tuple(1 if n == axis else key[n] for n in range(3))
                done[key], done[other] = vertex_pair(resid[key], resid[other])
        resid = done

    for i in range(2):
        for k in range(2):
            shift_buf[i, k, 0:1, :] = jnp.zeros((1, cells_z), jnp.float32)
            shift_buf[i, k, 1 : cells_y + 1, :] = resid[i, 1, k]
            main[i, k] = resid[i, 0, k] + shift_buf[i, k, 0:cells_y, :]
            top[i, k] = resid[i, 1, k][cells_y - 1 : cells_y, :]

    @pl.when(x == 0)
    def _():
        main_in[1] = jnp.zeros(main_in.shape[1:], jnp.float32)
        top_in[1] = jnp.zeros(top_in.shape[1:], jnp.float32)

    @pl.when(y == 0)
    def _():
        top_in[...] = jnp.zeros(top_in.shape, jnp.float32)

    def carry(number):
        to, ok_to, _, ok_from, i, j, source = carries[number]
        src, dst = (top, top_in) if j else (main, main_in)
        return (
            ok_to, ok_from, remote(src.at[i], dst.at[i, z], 12 + number, to),
            remote(src.at[i], dst.at[i, source], 12 + number, to),
        )

    for number in range(len(carries)):
        ok_to = carries[number][1]

        @pl.when(ok_to)
        def _(number=number):
            carry(number)[2].start()

    main_in[0, pl.ds(z, 1)] = main[0][None]

    for number in range(len(carries)):
        ok_from = carries[number][3]

        @pl.when(ok_from)
        def _(number=number):
            carry(number)[3].wait_recv()

    row = lax.broadcasted_iota(jnp.int32, (cells_y, cells_z), 0)
    column = lax.broadcasted_iota(jnp.int32, (cells_y, cells_z), 1)
    below = jnp.zeros((cells_y, cells_z), jnp.float32)
    for zz in range(nz):
        sums = []
        for k in range(2):
            total = main_in[0, zz, k] + main_in[1, zz, k]
            extra = top_in[0, zz, k] + top_in[1, zz, k]
            sums.append(total + jnp.where(row == 0, extra, 0.0))
        moved = pltpu.roll(jnp.where(column == cells_z - 1, below, sums[1]), 1, 1)
        below = sums[1]
        inside = (x > 0) & ((row > 0) | (y > 0))
        if zz == 0:
            inside = inside & (column > 0)
        coarse_ref[0, :, zz * cells_z : (zz + 1) * cells_z] = jnp.where(
            inside, sums[0] + moved, 0.0
        )

    for stage in range(2):
        for axis in range(3):
            over(finish, stage, axis)
    for number in range(len(carries)):
        ok_to = carries[number][1]

        @pl.when(ok_to)
        def _(number=number):
            carry(number)[2].wait_send()

    store.wait()


def per_device(sizes, rhs, orders):
    _, cells_y, cells_z = orders.shape
    nz = sizes[2]
    table = jnp.asarray(
        np.broadcast_to(
            (1.0 / (DIAGONAL * THETA))[:, :, :, None, None], DIAGONAL.shape + (1, cells_z)
        ),
        jnp.float32,
    )
    field = rhs.reshape(rhs.shape[:3] + rhs.shape[4:])
    cells = (cells_y, cells_z)
    rows = 8 * ((cells_y + 8) // 8)

    def buf(*shape):
        return pltpu.VMEM(shape, jnp.float32)

    def halo(n):
        line = (2, 2, n, n)
        return [
            buf(*line, *cells), buf(*line, *cells),
            buf(*line, 1, cells_z), buf(*line, 1, cells_z),
            buf(*line, *cells), buf(*line, *cells),
            buf(2, n, n, rows, cells_z), buf(2, n, n, rows, cells_z),
        ]

    slots = 12 + 4 * nz - 1
    vmem = pl.BlockSpec(memory_space=pltpu.VMEM)
    hbm = pl.BlockSpec(memory_space=pl.ANY)
    smoothed, coarse = pl.pallas_call(
        functools.partial(kernel, sizes, cells_y, cells_z),
        out_shape=(
            jax.ShapeDtypeStruct(field.shape, jnp.float32),
            jax.ShapeDtypeStruct((1, cells_y, nz * cells_z), jnp.float32),
        ),
        in_specs=[hbm, vmem, vmem],
        out_specs=(hbm, vmem),
        scratch_shapes=[buf(*field.shape)] * 4
        + halo(MODES)
        + halo(2)
        + [
            buf(2, 2, 2, *cells), buf(2, 2, rows, cells_z),
            buf(2, 2, *cells), buf(2, 2, 1, cells_z),
            buf(2, nz, 2, *cells), buf(2, nz, 2, 1, cells_z),
            pltpu.SemaphoreType.DMA((2,)),
            pltpu.SemaphoreType.DMA((slots,)),
            pltpu.SemaphoreType.DMA((slots,)),
        ],
        compiler_params=pltpu.CompilerParams(collective_id=0, has_side_effects=True),
        name="smoother",
    )(field, orders, table)
    return smoothed.reshape(rhs.shape), coarse


def solution(mesh):
    sizes = tuple(mesh.shape[axis] for axis in ("gx", "gy", "gz"))
    return jax.shard_map(
        functools.partial(per_device, sizes),
        mesh=mesh,
        in_specs=(P(None, None, None, "gx", "gy", "gz"), P("gx", "gy", "gz")),
        out_specs=(P(None, None, None, "gx", "gy", "gz"), P("gx", "gy", None)),
        check_vma=False,
    )
```

```python
import functools

import jax
import jax.numpy as jnp
import numpy as np
from jax import lax
from jax.experimental import pallas as pl
from jax.experimental.pallas import tpu as pltpu
from jax.sharding import PartitionSpec as P

PENALTY = 49.0
EIGEN_HIGH = 2.4
EIGEN_LOW = 0.24
MODES = 7
RELAYED = 3
MESH = pl.DeviceIdType.MESH


def tables():
    degree = np.arange(MODES)
    normed = np.sqrt((2.0 * degree + 1.0) / 2.0)
    smaller = np.minimum(degree[:, None], degree[None, :])
    parity = (degree[:, None] + degree[None, :]) % 2 == 0
    stiffness = np.where(parity, normed[:, None] * normed[None, :] * smaller * (smaller + 1), 0.0)
    signs = (-1.0) ** degree
    slope = normed * degree * (degree + 1) / 2.0
    low, low_slope = normed * signs, -slope * signs
    own = stiffness + np.outer(normed, PENALTY * normed - 0.5 * slope) - 0.5 * np.outer(slope, normed)
    own = own + np.outer(low, PENALTY * low + 0.5 * low_slope) + 0.5 * np.outer(low_slope, low)
    one_axis = normed * normed * degree * (degree + 1) + 2.0 * (
        PENALTY * normed * normed - normed * slope
    )
    diagonal = (
        one_axis[:, None, None] + one_axis[None, :, None] + one_axis[None, None, :]
    ) / PENALTY
    return (
        own / PENALTY,
        0.5 * slope - PENALTY * normed,
        0.5 * normed,
        normed / PENALTY,
        slope / PENALTY,
        diagonal,
    )


OWN, JUMP, HALF, VALUE, SLOPE, DIAGONAL = tables()
THETA = 0.5 * (EIGEN_HIGH + EIGEN_LOW)
DELTA = 0.5 * (EIGEN_HIGH - EIGEN_LOW)
RHO_FIRST = DELTA / THETA
RHO_SECOND = 1.0 / (2.0 * THETA / DELTA - RHO_FIRST)
KEEP = 1.0 + RHO_SECOND * RHO_FIRST
STEP = 2.0 * RHO_SECOND / DELTA * THETA


def combine(weights, values):
    total = None
    for weight, value in zip(weights, values):
        term = value * float(weight)
        total = term if total is None else total + term
    return total


def traces(values):
    even, odd = values[0::2], values[1::2]
    jump_even, jump_odd = combine(JUMP[0::2], even), combine(JUMP[1::2], odd)
    half_even, half_odd = combine(HALF[0::2], even), combine(HALF[1::2], odd)
    down = (jump_even - jump_odd, half_even - half_odd)
    up = (jump_even + jump_odd, half_even + half_odd)
    return down, up


def own_row(row, values):
    start = row % 2
    return combine(OWN[row, start::2], values[start::2])


def face_terms(from_up, from_down):
    both = (from_up[0] + from_down[0], from_up[1] + from_down[1])
    apart = (from_up[0] - from_down[0], from_up[1] - from_down[1])

    def term(mode):
        pair = both if mode % 2 == 0 else apart
        if mode == 0:
            return pair[0] * float(VALUE[0])
        return pair[0] * float(VALUE[mode]) + pair[1] * float(SLOPE[mode])

    return term


def vertex_pair(zero, one):
    flat, tilt = np.sqrt(0.5) * zero, (np.sqrt(1.5) / 3.0) * one
    return flat - tilt, flat + tilt


def kernel(
    sizes, cells_y, cells_z, rhs_hbm, orders_hbm, table_hbm, smooth, coarse_ref,
    rhs, first, acc, orders_ref, table_ref,
    xs, xr, ys, yr, zs, zr, y_up, y_down,
    xs2, xr2, ys2, yr2, zs2, zr2, y_up2, y_down2, acc2, shift_buf,
    main, top, main_in, top_in,
    relay, local_sem, send_sem, recv_sem, x_send, x_recv, relay_in, relay_out,
):
    nx, ny, nz = sizes
    x, y, z = lax.axis_index("gx"), lax.axis_index("gy"), lax.axis_index("gz")
    barrier = pltpu.get_barrier_semaphore()

    def neighbour(axis, sign):
        here = (x, y, z)[axis]
        to = [x, y, z]
        to[axis] = here + sign
        back = [x, y, z]
        back[axis] = here - sign
        below, above = here > 0, here < sizes[axis] - 1
        return (tuple(to), below if sign < 0 else above, tuple(back), above if sign < 0 else below)

    halos = [neighbour(axis, sign) for axis in range(3) for sign in (-1, 1)]
    always = x >= 0
    carries = []
    for i in range(2):
        for j in range(2):
            for r in range(nz):
                if i == 0 and j == 0 and r == 0:
                    continue
                to = (x + i, y + j, lax.rem(z + r, nz))
                source = lax.rem(z - r + nz, nz)
                back = (x - i, y - j, source)
                ok_to, ok_from = always, always
                if i:
                    ok_to, ok_from = ok_to & (x < nx - 1), ok_from & (x > 0)
                if j:
                    ok_to, ok_from = ok_to & (y < ny - 1), ok_from & (y > 0)
                carries.append((to, ok_to, back, ok_from, i, j, source))

    odd = lax.rem(x, 2) == 1
    even = jnp.logical_not(odd)
    relays = (
        ((x - 2, y, z), even & (x >= 2), (x + 2, y, z), even & (x + 2 < nx), (x + 1, y, z)),
        ((x + 2, y, z), odd & (x + 2 < nx), (x - 2, y, z), odd & (x >= 3), (x - 1, y, z)),
    )

    expected = jnp.int32(0)
    for entry in halos + list(relays) + carries:
        to, ok_to, back, ok_from = entry[:4]

        @pl.when(ok_from)
        def _(back=back):
            pl.semaphore_signal(barrier, inc=1, device_id=back, device_id_type=MESH)

        expected = expected + jnp.where(ok_to, 1, 0).astype(jnp.int32)

    loads = [
        pltpu.make_async_copy(orders_hbm, orders_ref, local_sem.at[MODES]),
        pltpu.make_async_copy(table_hbm, table_ref, local_sem.at[MODES + 1]),
    ]
    for copy in loads:
        copy.start()

    def rhs_load(b):
        return pltpu.make_async_copy(rhs_hbm.at[:, b], rhs.at[:, b], local_sem.at[b])

    for b in range(MODES):
        rhs_load(b).start()

    def remote(src, dst, slot, to):
        return pltpu.make_async_remote_copy(
            src_ref=src, dst_ref=dst, send_sem=send_sem.at[slot], recv_sem=recv_sem.at[slot],
            device_id=to, device_id_type=MESH,
        )

    def start(index, slot, src, dst):
        to, ok_to = halos[index][:2]

        @pl.when(ok_to)
        def _():
            remote(src, dst, slot, to).start()

    def receive(index, slot, src, dst):
        to, _, _, ok_from = halos[index]

        @pl.when(ok_from)
        def _():
            remote(src, dst, slot, to).wait_recv()

    def finish(index, slot, src, dst):
        to, ok_to = halos[index][:2]

        @pl.when(ok_to)
        def _():
            remote(src, dst, slot, to).wait_send()

    stages = (((xs, xr), (ys, yr), (zs, zr)), ((xs2, xr2), (ys2, yr2), (zs2, zr2)))

    def over(action, stage, axis):
        src, dst = stages[stage][axis]
        for side in range(2):
            index = 2 * axis + side
            action(index, 6 * stage + index, src.at[side], dst.at[side])

    for stage in range(2):
        for axis in range(3):
            for side in range(2):
                dst = stages[stage][axis][1]

                @pl.when(jnp.logical_not(halos[2 * axis + side][3]))
                def _(dst=dst, side=side):
                    dst[side] = jnp.zeros(dst.shape[1:], jnp.float32)

    for copy in loads:
        copy.wait()
    orders = orders_ref[0]
    tile = (MODES, cells_y, cells_z)
    last_mode = lax.broadcasted_iota(jnp.int32, tile, 0)
    lane = lax.broadcasted_iota(jnp.int32, (1, 1, cells_z), 2)

    def active(a, b):
        return jnp.maximum(jnp.maximum(a, b), last_mode) <= orders[None]

    def loop(body):
        def step(index, carry):
            body(index)
            return carry

        lax.fori_loop(0, MODES, step, 0)

    def x_copy(side, b, to):
        return pltpu.make_async_remote_copy(
            src_ref=xs.at[side, b], dst_ref=xr.at[side, b],
            send_sem=x_send.at[side, b], recv_sem=x_recv.at[side, b],
            device_id=to, device_id_type=MESH,
        )

    def to_relay(side, b, to):
        return pltpu.make_async_remote_copy(
            src_ref=xs.at[side, b], dst_ref=relay.at[side, b],
            send_sem=x_send.at[side, b], recv_sem=relay_in.at[side, b],
            device_id=to, device_id_type=MESH,
        )

    def from_relay(side, b, to):
        return pltpu.make_async_remote_copy(
            src_ref=relay.at[side, b], dst_ref=xr.at[side, b],
            send_sem=relay_out.at[side, b], recv_sem=x_recv.at[side, b],
            device_id=to, device_id_type=MESH,
        )

    def x_start(b):
        for side in range(2):
            to, ok_to = halos[side][:2]
            via, used = relays[side][:2]
            detour = used & (b < RELAYED)

            @pl.when(detour)
            def _():
                to_relay(side, b, via).start()

            @pl.when(ok_to & jnp.logical_not(detour))
            def _():
                x_copy(side, b, to).start()

    def forward(b):
        for side in range(2):
            back, relaying, target = relays[side][2:]

            @pl.when(relaying)
            def _():
                to_relay(side, b, target).wait_recv()
                from_relay(side, b, target).start()

    def x_receive(b):
        for side in range(2):

            @pl.when(halos[side][3])
            def _():
                x_copy(side, b, halos[side][0]).wait_recv()

    def x_finish(b):
        for side in range(2):

            @pl.when(halos[side][1])
            def _():
                x_copy(side, b, halos[side][0]).wait_send()

    def relay_finish(b):
        for side in range(2):

            @pl.when(relays[side][3])
            def _():
                from_relay(side, b, relays[side][4]).wait_send()

    pl.semaphore_wait(barrier, expected)

    def x_traces(b):
        rhs_load(b).wait()
        values = []
        for a in range(MODES):
            value = jnp.where(active(a, b), table_ref[a, b] * rhs[a, b], 0.0)
            first[a, b] = value
            values.append(value)
        sides = traces(values)
        for side in range(2):
            for kind in range(2):
                xs[side, b, kind] = sides[side][kind]
        x_start(b)

    loop(x_traces)

    def y_faces(a, values, send, up_buf, down_buf):
        down, up = traces(values)
        for kind in range(2):
            up_buf[kind, a, :, 0:cells_y, :] = down[kind]
            down_buf[kind, a, :, 1 : cells_y + 1, :] = up[kind]
            send[0, kind, a] = down[kind][:, 0:1, :]
            send[1, kind, a] = up[kind][:, cells_y - 1 : cells_y, :]

    def y_neighbours(a, received, up_buf, down_buf):
        for kind in range(2):
            up_buf[kind, a, :, cells_y : cells_y + 1, :] = received[0, kind, a]
            down_buf[kind, a, :, 0:1, :] = received[1, kind, a]
        return face_terms(
            [up_buf[kind, a, :, 1 : cells_y + 1, :] for kind in range(2)],
            [down_buf[kind, a, :, 0:cells_y, :] for kind in range(2)],
        )

    def z_faces(a, values, send):
        sides = traces(values)
        for side in range(2):
            for kind in range(2):
                send[side, kind, a] = sides[side][kind]

    def z_neighbours(a, send, received):
        def moved(side, kind, edge, amount):
            picked = jnp.where(lane == edge, received[side, kind, a], send[side, kind, a])
            return pltpu.roll(picked, amount, 2)

        return face_terms(
            [moved(0, kind, 0, cells_z - 1) for kind in range(2)],
            [moved(1, kind, cells_z - 1, 1) for kind in range(2)],
        )

    loop(lambda a: z_faces(a, [first[a, :, e] for e in range(MODES)], zs))
    over(start, 0, 2)
    loop(lambda a: y_faces(a, [first[a, b] for b in range(MODES)], ys, y_up, y_down))
    over(start, 0, 1)

    def x_own(b):
        values = [first[a, b] for a in range(MODES)]
        for a in range(MODES):
            acc[a, b] = own_row(a, values)

    def y_own(a):
        values = [first[a, b] for b in range(MODES)]
        for b in range(MODES):
            acc[a, b] += own_row(b, values)

    def z_own(a):
        values = [first[a, :, e] for e in range(MODES)]
        for e in range(MODES):
            acc[a, :, e] += own_row(e, values)

    loop(x_own)
    forward(0)
    loop(y_own)
    forward(1)
    loop(z_own)
    forward(2)

    over(receive, 0, 2)

    def z_flux(a):
        term = z_neighbours(a, zs, zr)
        for e in range(MODES):
            acc[a, :, e] += term(e)

    loop(z_flux)
    over(receive, 0, 1)

    def y_flux(a):
        term = y_neighbours(a, yr, y_up, y_down)
        for b in range(MODES):
            acc[a, b] += term(b)

    loop(y_flux)

    def x_flux(index):
        b = lax.rem(index + RELAYED, MODES)
        x_receive(b)
        term = face_terms(
            [xr[0, b, kind] for kind in range(2)], [xr[1, b, kind] for kind in range(2)]
        )
        for a in range(MODES):
            right = rhs[a, b]
            total = acc[a, b] + term(a)
            value = table_ref[a, b] * (KEEP * right + STEP * (right - total))
            smooth[a, b] = jnp.where(active(a, b), value, 0.0)

    loop(x_flux)

    for b in range(2):
        values = [smooth[a, b, 0:2] for a in range(MODES)]
        sides = traces(values)
        for side in range(2):
            for kind in range(2):
                xs2[side, kind, b] = sides[side][kind]
    over(start, 1, 0)
    for a in range(2):
        y_faces(a, [smooth[a, b, 0:2] for b in range(MODES)], ys2, y_up2, y_down2)
    over(start, 1, 1)
    for a in range(2):
        z_faces(a, [smooth[a, 0:2, e] for e in range(MODES)], zs2)
    over(start, 1, 2)
    for b in range(2):
        values = [smooth[a, b, 0:2] for a in range(MODES)]
        for a in range(2):
            acc2[a, b] = own_row(a, values)
    for a in range(2):
        values = [smooth[a, b, 0:2] for b in range(MODES)]
        for b in range(2):
            acc2[a, b] += own_row(b, values)
        values = [smooth[a, 0:2, e] for e in range(MODES)]
        for e in range(2):
            acc2[a, :, e] += own_row(e, values)
    over(receive, 1, 2)
    for a in range(2):
        term = z_neighbours(a, zs2, zr2)
        for e in range(2):
            acc2[a, :, e] += term(e)
    over(receive, 1, 1)
    for a in range(2):
        term = y_neighbours(a, yr2, y_up2, y_down2)
        for b in range(2):
            acc2[a, b] += term(b)
    over(receive, 1, 0)
    for b in range(2):
        term = face_terms(
            [xr2[0, kind, b] for kind in range(2)], [xr2[1, kind, b] for kind in range(2)]
        )
        for a in range(2):
            acc2[a, b] += term(a)

    resid = {}
    for a in range(2):
        for b in range(2):
            for e in range(2):
                left = rhs[a, b, e] - acc2[a, b, e]
                resid[a, b, e] = jnp.where(orders >= max(a, b, e), left, 0.0)
    for axis in range(3):
        done = {}
        for key in resid:
            if key[axis] == 0:
                other = tuple(1 if n == axis else key[n] for n in range(3))
                done[key], done[other] = vertex_pair(resid[key], resid[other])
        resid = done

    for i in range(2):
        for k in range(2):
            shift_buf[i, k, 0:1, :] = jnp.zeros((1, cells_z), jnp.float32)
            shift_buf[i, k, 1 : cells_y + 1, :] = resid[i, 1, k]
            main[i, k] = resid[i, 0, k] + shift_buf[i, k, 0:cells_y, :]
            top[i, k] = resid[i, 1, k][cells_y - 1 : cells_y, :]

    @pl.when(x == 0)
    def _():
        main_in[1] = jnp.zeros(main_in.shape[1:], jnp.float32)
        top_in[1] = jnp.zeros(top_in.shape[1:], jnp.float32)

    @pl.when(y == 0)
    def _():
        top_in[...] = jnp.zeros(top_in.shape, jnp.float32)

    def carry(number, arriving):
        to, _, _, _, i, j, source = carries[number]
        src, dst = (top, top_in) if j else (main, main_in)
        return remote(src.at[i], dst.at[i, source if arriving else z], 12 + number, to)

    for number in range(len(carries)):
        ok_to = carries[number][1]

        @pl.when(ok_to)
        def _(number=number):
            carry(number, False).start()

    main_in[0, pl.ds(z, 1)] = main[0][None]

    for number in range(len(carries)):
        ok_from = carries[number][3]

        @pl.when(ok_from)
        def _(number=number):
            carry(number, True).wait_recv()

    row = lax.broadcasted_iota(jnp.int32, (cells_y, cells_z), 0)
    column = lax.broadcasted_iota(jnp.int32, (cells_y, cells_z), 1)
    below = jnp.zeros((cells_y, cells_z), jnp.float32)
    for zz in range(nz):
        sums = []
        for k in range(2):
            total = main_in[0, zz, k] + main_in[1, zz, k]
            extra = top_in[0, zz, k] + top_in[1, zz, k]
            sums.append(total + jnp.where(row == 0, extra, 0.0))
        moved = pltpu.roll(jnp.where(column == cells_z - 1, below, sums[1]), 1, 1)
        below = sums[1]
        inside = (x > 0) & ((row > 0) | (y > 0))
        if zz == 0:
            inside = inside & (column > 0)
        coarse_ref[0, :, zz * cells_z : (zz + 1) * cells_z] = jnp.where(
            inside, sums[0] + moved, 0.0
        )

    for stage in range(2):
        for axis in range(3):
            if (stage, axis) != (0, 0):
                over(finish, stage, axis)
    loop(x_finish)
    for b in range(RELAYED):
        relay_finish(b)
    for number in range(len(carries)):
        ok_to = carries[number][1]

        @pl.when(ok_to)
        def _(number=number):
            carry(number, False).wait_send()


def per_device(sizes, rhs, orders):
    _, cells_y, cells_z = orders.shape
    nz = sizes[2]
    table = jnp.asarray(
        np.broadcast_to(
            (1.0 / (DIAGONAL * THETA))[:, :, :, None, None], DIAGONAL.shape + (1, cells_z)
        ),
        jnp.float32,
    )
    field = rhs.reshape(rhs.shape[:3] + rhs.shape[4:])
    cells = (cells_y, cells_z)
    rows = 8 * ((cells_y + 8) // 8)

    def buf(*shape):
        return pltpu.VMEM(shape, jnp.float32)

    def halo(n):
        line = (2, 2, n, n)
        x_line = (2, n, 2, n) if n == MODES else line
        return [
            buf(*x_line, *cells), buf(*x_line, *cells),
            buf(*line, 1, cells_z), buf(*line, 1, cells_z),
            buf(*line, *cells), buf(*line, *cells),
            buf(2, n, n, rows, cells_z), buf(2, n, n, rows, cells_z),
        ]

    slots = 12 + 4 * nz - 1
    vmem = pl.BlockSpec(memory_space=pltpu.VMEM)
    hbm = pl.BlockSpec(memory_space=pltpu.HBM)
    smoothed, coarse = pl.pallas_call(
        functools.partial(kernel, sizes, cells_y, cells_z),
        out_shape=(
            pltpu.VMEM(field.shape, jnp.float32),
            pltpu.VMEM((1, cells_y, nz * cells_z), jnp.float32),
        ),
        in_specs=[hbm, hbm, hbm],
        out_specs=(vmem, vmem),
        scratch_shapes=[buf(*field.shape)] * 3
        + [pltpu.VMEM(orders.shape, jnp.int32), buf(*table.shape)]
        + halo(MODES)
        + halo(2)
        + [
            buf(2, 2, 2, *cells), buf(2, 2, rows, cells_z),
            buf(2, 2, *cells), buf(2, 2, 1, cells_z),
            buf(2, nz, 2, *cells), buf(2, nz, 2, 1, cells_z),
            buf(2, RELAYED, 2, MODES, *cells),
            pltpu.SemaphoreType.DMA((MODES + 2,)),
            pltpu.SemaphoreType.DMA((slots,)),
            pltpu.SemaphoreType.DMA((slots,)),
            pltpu.SemaphoreType.DMA((2, MODES)),
            pltpu.SemaphoreType.DMA((2, MODES)),
            pltpu.SemaphoreType.DMA((2, RELAYED)),
            pltpu.SemaphoreType.DMA((2, RELAYED)),
        ],
        compiler_params=pltpu.CompilerParams(collective_id=0, has_side_effects=True, vmem_limit_bytes=24 * 2**20),
        name="smoother",
    )(field, orders, table)
    return smoothed.reshape(rhs.shape), coarse


def solution(mesh):
    sizes = tuple(mesh.shape[axis] for axis in ("gx", "gy", "gz"))
    return jax.shard_map(
        functools.partial(per_device, sizes),
        mesh=mesh,
        in_specs=(P(None, None, None, "gx", "gy", "gz"), P("gx", "gy", "gz")),
        out_specs=(P(None, None, None, "gx", "gy", "gz"), P("gx", "gy", None)),
        check_vma=False,
    )
```

```python
import functools

import jax
import jax.numpy as jnp
import numpy as np
from jax import lax
from jax.experimental import pallas as pl
from jax.experimental.pallas import tpu as pltpu
from jax.sharding import PartitionSpec as P

PENALTY = 49.0
EIGEN_HIGH = 2.4
EIGEN_LOW = 0.24
MODES = 7
RELAYED = 3
MESH = pl.DeviceIdType.MESH


def tables():
    degree = np.arange(MODES)
    normed = np.sqrt((2.0 * degree + 1.0) / 2.0)
    smaller = np.minimum(degree[:, None], degree[None, :])
    parity = (degree[:, None] + degree[None, :]) % 2 == 0
    stiffness = np.where(parity, normed[:, None] * normed[None, :] * smaller * (smaller + 1), 0.0)
    signs = (-1.0) ** degree
    slope = normed * degree * (degree + 1) / 2.0
    low, low_slope = normed * signs, -slope * signs
    own = stiffness + np.outer(normed, PENALTY * normed - 0.5 * slope) - 0.5 * np.outer(slope, normed)
    own = own + np.outer(low, PENALTY * low + 0.5 * low_slope) + 0.5 * np.outer(low_slope, low)
    one_axis = normed * normed * degree * (degree + 1) + 2.0 * (
        PENALTY * normed * normed - normed * slope
    )
    diagonal = (
        one_axis[:, None, None] + one_axis[None, :, None] + one_axis[None, None, :]
    ) / PENALTY
    return (
        own / PENALTY,
        0.5 * slope - PENALTY * normed,
        0.5 * normed,
        normed / PENALTY,
        slope / PENALTY,
        diagonal,
    )


OWN, JUMP, HALF, VALUE, SLOPE, DIAGONAL = tables()
THETA = 0.5 * (EIGEN_HIGH + EIGEN_LOW)
DELTA = 0.5 * (EIGEN_HIGH - EIGEN_LOW)
RHO_FIRST = DELTA / THETA
RHO_SECOND = 1.0 / (2.0 * THETA / DELTA - RHO_FIRST)
KEEP = 1.0 + RHO_SECOND * RHO_FIRST
STEP = 2.0 * RHO_SECOND / DELTA * THETA


def combine(weights, values):
    total = None
    for weight, value in zip(weights, values):
        term = value * float(weight)
        total = term if total is None else total + term
    return total


def traces(values):
    even, odd = values[0::2], values[1::2]
    jump_even, jump_odd = combine(JUMP[0::2], even), combine(JUMP[1::2], odd)
    half_even, half_odd = combine(HALF[0::2], even), combine(HALF[1::2], odd)
    down = (jump_even - jump_odd, half_even - half_odd)
    up = (jump_even + jump_odd, half_even + half_odd)
    return down, up


def own_row(row, values):
    start = row % 2
    return combine(OWN[row, start::2], values[start::2])


def face_terms(from_up, from_down):
    both = (from_up[0] + from_down[0], from_up[1] + from_down[1])
    apart = (from_up[0] - from_down[0], from_up[1] - from_down[1])

    def term(mode):
        pair = both if mode % 2 == 0 else apart
        if mode == 0:
            return pair[0] * float(VALUE[0])
        return pair[0] * float(VALUE[mode]) + pair[1] * float(SLOPE[mode])

    return term


def vertex_pair(zero, one):
    flat, tilt = np.sqrt(0.5) * zero, (np.sqrt(1.5) / 3.0) * one
    return flat - tilt, flat + tilt


def kernel(
    sizes, cells_y, cells_z, rhs_hbm, orders_hbm, table_hbm, smooth, coarse_ref,
    rhs, first, acc, orders_ref, table_ref,
    xs, xr, ys, yr, zs, zr, y_up, y_down,
    xs2, xr2, ys2, yr2, zs2, zr2, y_up2, y_down2, acc2, shift_buf,
    main, top, main_in, top_in,
    relay, local_sem, send_sem, recv_sem, x_send, x_recv, relay_in, relay_out,
):
    nx, ny, nz = sizes
    x, y, z = lax.axis_index("gx"), lax.axis_index("gy"), lax.axis_index("gz")
    barrier = pltpu.get_barrier_semaphore()

    def neighbour(axis, sign):
        here = (x, y, z)[axis]
        to = [x, y, z]
        to[axis] = here + sign
        back = [x, y, z]
        back[axis] = here - sign
        below, above = here > 0, here < sizes[axis] - 1
        return (tuple(to), below if sign < 0 else above, tuple(back), above if sign < 0 else below)

    halos = [neighbour(axis, sign) for axis in range(3) for sign in (-1, 1)]
    always = x >= 0
    carries = []
    for i in range(2):
        for j in range(2):
            for r in range(nz):
                if i == 0 and j == 0 and r == 0:
                    continue
                to = (x + i, y + j, lax.rem(z + r, nz))
                source = lax.rem(z - r + nz, nz)
                back = (x - i, y - j, source)
                ok_to, ok_from = always, always
                if i:
                    ok_to, ok_from = ok_to & (x < nx - 1), ok_from & (x > 0)
                if j:
                    ok_to, ok_from = ok_to & (y < ny - 1), ok_from & (y > 0)
                carries.append((to, ok_to, back, ok_from, i, j, source))

    odd = lax.rem(x, 2) == 1
    even = jnp.logical_not(odd)
    relays = (
        ((x - 2, y, z), even & (x >= 2), (x + 2, y, z), even & (x + 2 < nx), (x + 1, y, z)),
        ((x + 2, y, z), odd & (x + 2 < nx), (x - 2, y, z), odd & (x >= 3), (x - 1, y, z)),
    )

    expected = jnp.int32(0)
    for entry in halos + list(relays):
        to, ok_to, back, ok_from = entry[:4]

        @pl.when(ok_from)
        def _(back=back):
            pl.semaphore_signal(barrier, inc=1, device_id=back, device_id_type=MESH)

        expected = expected + jnp.where(ok_to, 1, 0).astype(jnp.int32)

    loads = [
        pltpu.make_async_copy(orders_hbm, orders_ref, local_sem.at[MODES]),
        pltpu.make_async_copy(table_hbm, table_ref, local_sem.at[MODES + 1]),
    ]
    for copy in loads:
        copy.start()

    def rhs_load(b):
        return pltpu.make_async_copy(rhs_hbm.at[:, b], rhs.at[:, b], local_sem.at[b])

    for b in range(MODES):
        rhs_load(b).start()

    def remote(src, dst, slot, to):
        return pltpu.make_async_remote_copy(
            src_ref=src, dst_ref=dst, send_sem=send_sem.at[slot], recv_sem=recv_sem.at[slot],
            device_id=to, device_id_type=MESH,
        )

    def start(index, slot, src, dst):
        to, ok_to = halos[index][:2]

        @pl.when(ok_to)
        def _():
            remote(src, dst, slot, to).start()

    def receive(index, slot, src, dst):
        to, _, _, ok_from = halos[index]

        @pl.when(ok_from)
        def _():
            remote(src, dst, slot, to).wait_recv()

    def finish(index, slot, src, dst):
        to, ok_to = halos[index][:2]

        @pl.when(ok_to)
        def _():
            remote(src, dst, slot, to).wait_send()

    stages = (((xs, xr), (ys, yr), (zs, zr)), ((xs2, xr2), (ys2, yr2), (zs2, zr2)))

    def over(action, stage, axis):
        src, dst = stages[stage][axis]
        for side in range(2):
            index = 2 * axis + side
            action(index, 6 * stage + index, src.at[side], dst.at[side])

    for stage in range(2):
        for axis in range(3):
            for side in range(2):
                dst = stages[stage][axis][1]

                @pl.when(jnp.logical_not(halos[2 * axis + side][3]))
                def _(dst=dst, side=side):
                    dst[side] = jnp.zeros(dst.shape[1:], jnp.float32)

    for copy in loads:
        copy.wait()
    orders = orders_ref[0]
    tile = (MODES, cells_y, cells_z)
    last_mode = lax.broadcasted_iota(jnp.int32, tile, 0)
    lane = lax.broadcasted_iota(jnp.int32, (1, 1, cells_z), 2)

    def active(a, b):
        return jnp.maximum(jnp.maximum(a, b), last_mode) <= orders[None]

    def loop(body):
        def step(index, carry):
            body(index)
            return carry

        lax.fori_loop(0, MODES, step, 0)

    def x_copy(side, b, to):
        return pltpu.make_async_remote_copy(
            src_ref=xs.at[side, b], dst_ref=xr.at[side, b],
            send_sem=x_send.at[side, b], recv_sem=x_recv.at[side, b],
            device_id=to, device_id_type=MESH,
        )

    def to_relay(side, b, to):
        return pltpu.make_async_remote_copy(
            src_ref=xs.at[side, b], dst_ref=relay.at[side, b],
            send_sem=x_send.at[side, b], recv_sem=relay_in.at[side, b],
            device_id=to, device_id_type=MESH,
        )

    def from_relay(side, b, to):
        return pltpu.make_async_remote_copy(
            src_ref=relay.at[side, b], dst_ref=xr.at[side, b],
            send_sem=relay_out.at[side, b], recv_sem=x_recv.at[side, b],
            device_id=to, device_id_type=MESH,
        )

    def x_start(b):
        for side in range(2):
            to, ok_to = halos[side][:2]
            via, used = relays[side][:2]
            detour = used & (b < RELAYED)

            @pl.when(detour)
            def _():
                to_relay(side, b, via).start()

            @pl.when(ok_to & jnp.logical_not(detour))
            def _():
                x_copy(side, b, to).start()

    def forward(b):
        for side in range(2):
            back, relaying, target = relays[side][2:]

            @pl.when(relaying)
            def _():
                to_relay(side, b, target).wait_recv()
                from_relay(side, b, target).start()

    def x_receive(b):
        for side in range(2):

            @pl.when(halos[side][3])
            def _():
                x_copy(side, b, halos[side][0]).wait_recv()

    def x_finish(b):
        for side in range(2):

            @pl.when(halos[side][1])
            def _():
                x_copy(side, b, halos[side][0]).wait_send()

    def relay_finish(b):
        for side in range(2):

            @pl.when(relays[side][3])
            def _():
                from_relay(side, b, relays[side][4]).wait_send()

    pl.semaphore_wait(barrier, expected)

    def x_traces(b):
        rhs_load(b).wait()
        values = []
        for a in range(MODES):
            value = jnp.where(active(a, b), table_ref[a, b] * rhs[a, b], 0.0)
            first[a, b] = value
            values.append(value)
        sides = traces(values)
        for side in range(2):
            for kind in range(2):
                xs[side, b, kind] = sides[side][kind]
        x_start(b)

    loop(x_traces)

    def y_faces(a, values, send, up_buf, down_buf):
        down, up = traces(values)
        for kind in range(2):
            up_buf[kind, a, :, 0:cells_y, :] = down[kind]
            down_buf[kind, a, :, 1 : cells_y + 1, :] = up[kind]
            send[0, kind, a] = down[kind][:, 0:1, :]
            send[1, kind, a] = up[kind][:, cells_y - 1 : cells_y, :]

    def y_neighbours(a, received, up_buf, down_buf):
        for kind in range(2):
            up_buf[kind, a, :, cells_y : cells_y + 1, :] = received[0, kind, a]
            down_buf[kind, a, :, 0:1, :] = received[1, kind, a]
        return face_terms(
            [up_buf[kind, a, :, 1 : cells_y + 1, :] for kind in range(2)],
            [down_buf[kind, a, :, 0:cells_y, :] for kind in range(2)],
        )

    def z_faces(a, values, send):
        sides = traces(values)
        for side in range(2):
            for kind in range(2):
                send[side, kind, a] = sides[side][kind]

    def z_neighbours(a, send, received):
        def moved(side, kind, edge, amount):
            picked = jnp.where(lane == edge, received[side, kind, a], send[side, kind, a])
            return pltpu.roll(picked, amount, 2)

        return face_terms(
            [moved(0, kind, 0, cells_z - 1) for kind in range(2)],
            [moved(1, kind, cells_z - 1, 1) for kind in range(2)],
        )

    loop(lambda a: z_faces(a, [first[a, :, e] for e in range(MODES)], zs))
    over(start, 0, 2)
    loop(lambda a: y_faces(a, [first[a, b] for b in range(MODES)], ys, y_up, y_down))
    over(start, 0, 1)

    def x_own(b):
        values = [first[a, b] for a in range(MODES)]
        for a in range(MODES):
            acc[a, b] = own_row(a, values)

    def y_own(a):
        values = [first[a, b] for b in range(MODES)]
        for b in range(MODES):
            acc[a, b] += own_row(b, values)

    def z_own(a):
        values = [first[a, :, e] for e in range(MODES)]
        for e in range(MODES):
            acc[a, :, e] += own_row(e, values)

    loop(x_own)
    forward(0)
    loop(y_own)
    forward(1)
    loop(z_own)
    forward(2)

    over(receive, 0, 2)

    def z_flux(a):
        term = z_neighbours(a, zs, zr)
        for e in range(MODES):
            acc[a, :, e] += term(e)

    loop(z_flux)
    over(receive, 0, 1)

    def y_flux(a):
        term = y_neighbours(a, yr, y_up, y_down)
        for b in range(MODES):
            acc[a, b] += term(b)

    loop(y_flux)

    def x_flux(index):
        b = lax.rem(index + RELAYED, MODES)
        x_receive(b)
        term = face_terms(
            [xr[0, b, kind] for kind in range(2)], [xr[1, b, kind] for kind in range(2)]
        )
        for a in range(MODES):
            right = rhs[a, b]
            total = acc[a, b] + term(a)
            value = table_ref[a, b] * (KEEP * right + STEP * (right - total))
            smooth[a, b] = jnp.where(active(a, b), value, 0.0)

    loop(x_flux)

    for b in range(2):
        values = [smooth[a, b, 0:2] for a in range(MODES)]
        sides = traces(values)
        for side in range(2):
            for kind in range(2):
                xs2[side, kind, b] = sides[side][kind]
    over(start, 1, 0)
    for a in range(2):
        y_faces(a, [smooth[a, b, 0:2] for b in range(MODES)], ys2, y_up2, y_down2)
    over(start, 1, 1)
    for a in range(2):
        z_faces(a, [smooth[a, 0:2, e] for e in range(MODES)], zs2)
    over(start, 1, 2)
    for b in range(2):
        values = [smooth[a, b, 0:2] for a in range(MODES)]
        for a in range(2):
            acc2[a, b] = own_row(a, values)
    for a in range(2):
        values = [smooth[a, b, 0:2] for b in range(MODES)]
        for b in range(2):
            acc2[a, b] += own_row(b, values)
        values = [smooth[a, 0:2, e] for e in range(MODES)]
        for e in range(2):
            acc2[a, :, e] += own_row(e, values)
    over(receive, 1, 2)
    for a in range(2):
        term = z_neighbours(a, zs2, zr2)
        for e in range(2):
            acc2[a, :, e] += term(e)
    over(receive, 1, 1)
    for a in range(2):
        term = y_neighbours(a, yr2, y_up2, y_down2)
        for b in range(2):
            acc2[a, b] += term(b)
    over(receive, 1, 0)
    for b in range(2):
        term = face_terms(
            [xr2[0, kind, b] for kind in range(2)], [xr2[1, kind, b] for kind in range(2)]
        )
        for a in range(2):
            acc2[a, b] += term(a)

    resid = {}
    for a in range(2):
        for b in range(2):
            for e in range(2):
                left = rhs[a, b, e] - acc2[a, b, e]
                resid[a, b, e] = jnp.where(orders >= max(a, b, e), left, 0.0)
    for axis in range(3):
        done = {}
        for key in resid:
            if key[axis] == 0:
                other = tuple(1 if n == axis else key[n] for n in range(3))
                done[key], done[other] = vertex_pair(resid[key], resid[other])
        resid = done

    for i in range(2):
        for k in range(2):
            shift_buf[i, k, 0:1, :] = jnp.zeros((1, cells_z), jnp.float32)
            shift_buf[i, k, 1 : cells_y + 1, :] = resid[i, 1, k]
            main[i, k] = resid[i, 0, k] + shift_buf[i, k, 0:cells_y, :]
            top[i, k] = resid[i, 1, k][cells_y - 1 : cells_y, :]

    @pl.when(x == 0)
    def _():
        main_in[1] = jnp.zeros(main_in.shape[1:], jnp.float32)
        top_in[1] = jnp.zeros(top_in.shape[1:], jnp.float32)

    @pl.when(y == 0)
    def _():
        top_in[...] = jnp.zeros(top_in.shape, jnp.float32)

    def carry(number, arriving):
        to, _, _, _, i, j, source = carries[number]
        src, dst = (top, top_in) if j else (main, main_in)
        return remote(src.at[i], dst.at[i, source if arriving else z], 12 + number, to)

    for number in range(len(carries)):
        ok_to = carries[number][1]

        @pl.when(ok_to)
        def _(number=number):
            carry(number, False).start()

    main_in[0, pl.ds(z, 1)] = main[0][None]

    for number in range(len(carries)):
        ok_from = carries[number][3]

        @pl.when(ok_from)
        def _(number=number):
            carry(number, True).wait_recv()

    row = lax.broadcasted_iota(jnp.int32, (cells_y, cells_z), 0)
    column = lax.broadcasted_iota(jnp.int32, (cells_y, cells_z), 1)
    below = jnp.zeros((cells_y, cells_z), jnp.float32)
    for zz in range(nz):
        sums = []
        for k in range(2):
            total = main_in[0, zz, k] + main_in[1, zz, k]
            extra = top_in[0, zz, k] + top_in[1, zz, k]
            sums.append(total + jnp.where(row == 0, extra, 0.0))
        moved = pltpu.roll(jnp.where(column == cells_z - 1, below, sums[1]), 1, 1)
        below = sums[1]
        inside = (x > 0) & ((row > 0) | (y > 0))
        if zz == 0:
            inside = inside & (column > 0)
        coarse_ref[0, :, zz * cells_z : (zz + 1) * cells_z] = jnp.where(
            inside, sums[0] + moved, 0.0
        )

    for stage in range(2):
        for axis in range(3):
            if (stage, axis) != (0, 0):
                over(finish, stage, axis)
    loop(x_finish)
    for b in range(RELAYED):
        relay_finish(b)
    for number in range(len(carries)):
        ok_to = carries[number][1]

        @pl.when(ok_to)
        def _(number=number):
            carry(number, False).wait_send()


def per_device(sizes, rhs, orders):
    _, cells_y, cells_z = orders.shape
    nz = sizes[2]
    table = jnp.asarray(
        np.broadcast_to(
            (1.0 / (DIAGONAL * THETA))[:, :, :, None, None], DIAGONAL.shape + (1, cells_z)
        ),
        jnp.float32,
    )
    field = rhs.reshape(rhs.shape[:3] + rhs.shape[4:])
    cells = (cells_y, cells_z)
    rows = 8 * ((cells_y + 8) // 8)

    def buf(*shape):
        return pltpu.VMEM(shape, jnp.float32)

    def halo(n):
        line = (2, 2, n, n)
        x_line = (2, n, 2, n) if n == MODES else line
        return [
            buf(*x_line, *cells), buf(*x_line, *cells),
            buf(*line, 1, cells_z), buf(*line, 1, cells_z),
            buf(*line, *cells), buf(*line, *cells),
            buf(2, n, n, rows, cells_z), buf(2, n, n, rows, cells_z),
        ]

    slots = 12 + 4 * nz - 1
    vmem = pl.BlockSpec(memory_space=pltpu.VMEM)
    hbm = pl.BlockSpec(memory_space=pltpu.HBM)
    smoothed, coarse = pl.pallas_call(
        functools.partial(kernel, sizes, cells_y, cells_z),
        out_shape=(
            pltpu.VMEM(field.shape, jnp.float32),
            pltpu.VMEM((1, cells_y, nz * cells_z), jnp.float32),
        ),
        in_specs=[hbm, hbm, hbm],
        out_specs=(vmem, vmem),
        scratch_shapes=[buf(*field.shape)] * 3
        + [pltpu.VMEM(orders.shape, jnp.int32), buf(*table.shape)]
        + halo(MODES)
        + halo(2)
        + [
            buf(2, 2, 2, *cells), buf(2, 2, rows, cells_z),
            buf(2, 2, *cells), buf(2, 2, 1, cells_z),
            buf(2, nz, 2, *cells), buf(2, nz, 2, 1, cells_z),
            buf(2, RELAYED, 2, MODES, *cells),
            pltpu.SemaphoreType.DMA((MODES + 2,)),
            pltpu.SemaphoreType.DMA((slots,)),
            pltpu.SemaphoreType.DMA((slots,)),
            pltpu.SemaphoreType.DMA((2, MODES)),
            pltpu.SemaphoreType.DMA((2, MODES)),
            pltpu.SemaphoreType.DMA((2, RELAYED)),
            pltpu.SemaphoreType.DMA((2, RELAYED)),
        ],
        compiler_params=pltpu.CompilerParams(collective_id=0, has_side_effects=True),
        name="smoother",
    )(field, orders, table)
    return smoothed.reshape(rhs.shape), coarse


def solution(mesh):
    sizes = tuple(mesh.shape[axis] for axis in ("gx", "gy", "gz"))
    return jax.shard_map(
        functools.partial(per_device, sizes),
        mesh=mesh,
        in_specs=(P(None, None, None, "gx", "gy", "gz"), P("gx", "gy", "gz")),
        out_specs=(P(None, None, None, "gx", "gy", "gz"), P("gx", "gy", None)),
        check_vma=False,
    )
```
